256 devices in a mesh: row: 4 (over x_hi, core), col: 4 (over y), layer: 16 (over z, x_lo).
Axes of the slice: x: 4 (x_hi: 2, x_lo: 2; x = x_hi * 2 + x_lo), y: 4, z: 8, core: 2. Of those that a mesh axis runs over, the one named last changes fastest.
Arguments:
- blocks: bfloat16 [16, 4, 64, 12, 4096], P(None, 'col', 'row', None, 'layer'), may hold values from -6 to 6
- grid_class: int32 [64], replicated, may hold values from 0 to 63, each once
- neighbor: int32 [64, 64, 12], replicated, may hold values from 0 to 11, as said below
Outputs:
- updated: bfloat16 [4, 64, 12, 4096], P('col', 'row', None, 'layer')
The draws below stay inside these ranges and needn't reach their ends.
Inputs may be any that keep to these rules, and one draw needn't show every extreme that they name: `grid_class`: a permutation. neighbor[r, a, m] is the member of class a to which member m of class r is coupled; every block is coupled to exactly one member of each class, and to itself within its own class.
All inputs are finite; a program needn't handle non-finite values.
Results may differ from the reference program's by a relative error of at most 0.007.
Values may be sent and summed in bfloat16 or wider, within the bound.
A program may use at most 128 MiB of HBM per device.

```python
import math
import jax
import jax.numpy as jnp
from jax import lax

LX = 8
LY = 8
LZ = 12
BS = 64
NCLS = 64
WIN = 4
MEM = 12
N_LAYER = 16


def reach_member(coordinate, offsets, extent, residue):
    window_begin = coordinate + offsets[..., None]
    return jnp.mod(window_begin + jnp.mod(residue - window_begin, 4), extent) // 4


def draw_neighbor(key, part):
    starts = jax.random.randint(key, (LX, LY, LZ, 3), 0, 2).astype(jnp.int32) - 2
    residue = jnp.arange(4, dtype=jnp.int32)[None, None, None, :]
    cells_x = jnp.arange(LX, dtype=jnp.int32)[:, None, None, None]
    cells_y = jnp.arange(LY, dtype=jnp.int32)[None, :, None, None]
    cells_z = jnp.arange(LZ, dtype=jnp.int32)[None, None, :, None]
    member_x = reach_member(cells_x, starts[..., 0], LX, residue)
    member_y = reach_member(cells_y, starts[..., 1], LY, residue)
    member_z = reach_member(cells_z, starts[..., 2], LZ, residue)
    members = (member_x[..., :, None, None] * (LY // 4) + member_y[..., None, :, None]) * (LZ // 4) + member_z[..., None, None, :]
    members = members.reshape(LX // 4, 4, LY // 4, 4, LZ // 4, 4, 64)
    members = jnp.transpose(members, (1, 3, 5, 6, 0, 2, 4))
    return members.reshape(NCLS, NCLS, MEM).astype(jnp.int32)


def block_levels(key, dims, split, least, top_value):
    def one(dim, shards_of):
        draws = jax.random.uniform(jax.random.fold_in(jax.random.fold_in(key, 6), dim), (shards_of,), jnp.float32, least / len(split), top_value / len(split))
        return jnp.repeat(jnp.exp(draws), dims[dim] // shards_of).reshape((-1,) + (1,) * (len(dims) - dim - 1))

    level = one(*split[0])
    for cut in split[1:]:
        level = level * one(*cut)
    return level


def centred(own_key, dims, scale, reach, split=(), held_as=jnp.bfloat16):
    level = block_levels(own_key, dims, split, -0.22, 0.18) if split else 1.0
    entries = jax.random.normal(own_key, dims, jnp.float32) * scale * level
    return jnp.minimum(jnp.maximum(entries, -reach), reach).astype(held_as)


def setup_inputs(seed: int = 0) -> dict:
    keys = jax.random.split(jax.random.key(seed), 4)
    blocks = centred(keys[0], (NCLS // WIN, WIN, NCLS, MEM, BS * BS), 1.0, 6.0, ((1, 4), (2, 4), (4, 16)))
    grid_class = jax.random.permutation(keys[1], NCLS).astype(jnp.int32)
    neighbor = draw_neighbor(jax.random.fold_in(keys[3], 71), 0)
    return dict(blocks=blocks, grid_class=grid_class, neighbor=neighbor)


def product(left_rows, matrix, partner, scaling):
    inner = BS // N_LAYER

    def one_row(inputs):
        row_blocks, row_partner = inputs

        def accumulate(running, position):
            partner_members = row_partner[position]
            chosen = matrix[position][:, partner_members]
            coupled = partner[position][:, partner_members]
            retain = (coupled == row_partner).astype(jnp.float32)
            left_part = row_blocks[position].astype(jnp.float32).reshape(MEM, BS, N_LAYER, inner)
            right_part = chosen.astype(jnp.float32).reshape(NCLS, MEM, N_LAYER, inner, BS)
            term = jnp.einsum('mple,qmleo->lqmpo', left_part, right_part)
            return (running + term * retain[None, :, :, None, None], None)
        zeroed = jnp.zeros((N_LAYER, NCLS, MEM, BS, BS), jnp.float32)
        running, unused = lax.scan(accumulate, zeroed, jnp.arange(NCLS, dtype=jnp.int32))
        rounded = lax.optimization_barrier(running.astype(jnp.bfloat16)).astype(jnp.float32)
        return scaling * lax.optimization_barrier(jnp.sum(rounded, axis=0))
    return lax.map(one_row, (left_rows, partner[:WIN]))

def reference(blocks, grid_class, neighbor):
    partner = neighbor[grid_class[:, None], grid_class[None, :]]
    scaling = 1.0 / math.sqrt(NCLS * BS)
    matrix = blocks.reshape(NCLS, NCLS, MEM, BS, BS)
    window_rows = matrix[:WIN]
    square = product(window_rows, matrix, partner, scaling).astype(jnp.bfloat16)
    cubed = product(square, matrix, partner, scaling)
    updated = 1.5 * window_rows.astype(jnp.float32) - 0.5 * cubed
    return updated.astype(jnp.bfloat16).reshape(WIN, NCLS, MEM, BS * BS)
```

```python
import functools
import math

import jax
import jax.numpy as jnp
from jax import lax
from jax.experimental import pallas as pl
from jax.experimental.pallas import tpu as pltpu
from jax.sharding import PartitionSpec as P

BS = 64
NCLS = 64
WIN = 4
MEM = 12
PAIRS = MEM // 2
NZ = 8
NX = 8
NY = 4
QH = 8
SCALE = 1.0 / math.sqrt(NCLS * BS)
MESH = pl.DeviceIdType.MESH
F32 = jnp.float32
BF16 = jnp.bfloat16
VMEM = pl.BlockSpec(memory_space=pltpu.VMEM)
HBM = pl.BlockSpec(memory_space=pl.ANY)
SMEM = pl.BlockSpec(memory_space=pltpu.SMEM)


def contract(a, b, da, db):
    return lax.dot_general(a, b, (((da,), (db,)), ((), ())), preferred_element_type=F32)


def tables_kernel(gcol_ref, neigh_ref, mu_ref, mask_ref, part_ref, col_ref):
    mine = lax.axis_index("col")
    lanes = lax.broadcasted_iota(jnp.int32, (NCLS, NCLS), 1)
    rows = lax.broadcasted_iota(jnp.int32, (NCLS, NCLS), 0)
    place = (gcol_ref[...] == lanes).astype(F32)
    own_row = contract((lax.broadcasted_iota(jnp.int32, (8, NCLS), 1) == mine).astype(F32), place, 1, 0)[0:1]
    for m in range(MEM):
        table = neigh_ref[m].astype(F32)
        half = contract(place, table, 1, 1)
        col_ref[m] = jnp.sum(half * own_row, axis=1, keepdims=True)
        full = contract(place, half, 1, 1)
        part_ref[m] = full
    row_on = rows == mine
    for m in range(MEM):
        target = jnp.sum(jnp.where(row_on, part_ref[m], 0.0), axis=0, keepdims=True)
        mu_ref[m : m + 1, :] = target.astype(jnp.int32)
        column = col_ref[m]
        coupled = jnp.zeros((NCLS, NCLS), F32)
        for other in range(MEM):
            coupled = jnp.where(column == other, part_ref[other], coupled)
        mask_ref[m] = (coupled == target).astype(F32)


def tables(grid_class, neighbor):
    return pl.pallas_call(
        tables_kernel,
        out_shape=(
            jax.ShapeDtypeStruct((MEM, NCLS), jnp.int32),
            jax.ShapeDtypeStruct((MEM, NCLS, NCLS), F32),
        ),
        in_specs=[VMEM, VMEM],
        out_specs=(VMEM, VMEM),
        scratch_shapes=[pltpu.VMEM((MEM, NCLS, NCLS), F32), pltpu.VMEM((MEM, NCLS, 1), F32)],
    )(grid_class[:, None], jnp.transpose(neighbor, (2, 0, 1)))


def greet(peers):
    barrier = pltpu.get_barrier_semaphore()
    for peer in peers:
        pl.semaphore_signal(barrier, inc=1, device_id=peer, device_id_type=MESH)
    pl.semaphore_wait(barrier, len(peers))


def plane_peers():
    row = lax.axis_index("row")
    layer = lax.axis_index("layer")
    half = lax.rem(layer, 2)
    slot = row * 2 + half
    peers = []
    for offset in range(1, NX):
        other = lax.rem(slot + offset, NX)
        peers.append({"row": other // 2, "layer": layer - half + lax.rem(other, 2)})
    return slot, peers


def gather_kernel(x_ref, y_ref, xg_ref, yg_ref, xsend, xrecv, ysend, yrecv):
    mine = lax.axis_index("col")
    right = {"col": lax.rem(mine + 1, NY)}
    left = {"col": lax.rem(mine + NY - 1, NY)}
    slot, peers = plane_peers()
    greet([right, left] + peers)
    lo, hi = pl.ds(0, 8), pl.ds(8, 8)

    def copy(src, dst, index, peer):
        return pltpu.make_async_remote_copy(
            src_ref=src, dst_ref=dst, send_sem=xsend.at[index], recv_sem=xrecv.at[index],
            device_id=peer, device_id_type=MESH,
        )

    first = [
        copy(x_ref.at[lo], xg_ref.at[0, lo], 0, right),
        copy(x_ref.at[hi], xg_ref.at[1, hi], 1, left),
        copy(x_ref.at[hi], xg_ref.at[0, hi], 2, right),
        copy(x_ref.at[lo], xg_ref.at[1, lo], 3, left),
    ]
    forward = [
        copy(xg_ref.at[0, lo], xg_ref.at[2, lo], 4, right),
        copy(xg_ref.at[1, hi], xg_ref.at[2, hi], 5, left),
    ]
    for one in first:
        one.start()
    sends = []
    for index, peer in enumerate(peers):
        one = pltpu.make_async_remote_copy(
            src_ref=y_ref, dst_ref=yg_ref.at[slot], send_sem=ysend.at[index], recv_sem=yrecv.at[index],
            device_id=peer, device_id_type=MESH,
        )
        one.start()
        sends.append(one)
    yg_ref[slot] = y_ref[...]
    first[0].wait_recv()
    forward[0].start()
    first[1].wait_recv()
    forward[1].start()
    for one in sends:
        one.wait()
    first[0].wait_send()
    first[1].wait_send()
    for one in first[2:] + forward:
        one.wait()


def gather(x, y):
    return pl.pallas_call(
        gather_kernel,
        out_shape=(
            jax.ShapeDtypeStruct((3,) + x.shape, BF16),
            jax.ShapeDtypeStruct((NX,) + y.shape, BF16),
        ),
        in_specs=[HBM, VMEM],
        out_specs=(HBM, VMEM),
        scratch_shapes=[
            pltpu.SemaphoreType.DMA((6,)),
            pltpu.SemaphoreType.DMA((6,)),
            pltpu.SemaphoreType.DMA((NX - 1,)),
            pltpu.SemaphoreType.DMA((NX - 1,)),
        ],
        compiler_params=pltpu.CompilerParams(collective_id=0, has_side_effects=True),
    )(x, y)


def first_kernel(mu_ref, mask_ref, own_ref, xg_ref, y_ref, chosen_ref, out_ref, xs, spread, sems):
    pair = pl.program_id(0)
    mine = lax.axis_index("col")

    @pl.when(pair == 0)
    def _():
        copies = [pltpu.make_async_copy(own_ref, xs.at[mine], sems.at[0])]
        for slot, offset in enumerate((3, 1, 2)):
            copies.append(
                pltpu.make_async_copy(xg_ref.at[slot], xs.at[lax.rem(mine + offset, NY)], sems.at[slot + 1])
            )
        for one in copies:
            one.start()
        for one in copies:
            one.wait()

    base = lax.axis_index("row") * 16 + lax.rem(lax.axis_index("layer"), 2) * QH
    lane = lax.broadcasted_iota(jnp.int32, (NCLS, QH * BS), 1) // BS
    row = lax.broadcasted_iota(jnp.int32, (NCLS, QH * BS), 0)
    expand = (row == lane + base).astype(F32)
    left = y_ref[...].reshape(NCLS * 8, 128).T
    for which in range(2):
        m = pair * 2 + which
        spread[...] = contract(mask_ref[which], expand, 1, 0)

        def step(h, carry):
            for w in range(NY):
                a = h * NY + w
                block = xs[w, h, mu_ref[m, a]].astype(F32)
                kept = block * spread[pl.ds(a, 1), :]
                chosen_ref[which, pl.ds(pl.multiple_of(a * 8, 8), 8), :] = kept.astype(BF16)
            return carry

        lax.fori_loop(0, 16, step, 0)
    top = contract(left[:BS], chosen_ref[0], 1, 0)
    low = contract(left[BS:], chosen_ref[1], 1, 0)
    total = jnp.concatenate([top, low], axis=0).T
    total = total.reshape(QH, NZ, 8, 128)
    for z in range(NZ):
        out_ref[z, 0] = total[:, z].reshape(QH * 8, 128).astype(BF16)


def first_product(mu, mask, own, xg, y):
    return pl.pallas_call(
        first_kernel,
        grid=(PAIRS,),
        out_shape=(
            jax.ShapeDtypeStruct((MEM, NCLS * 8, QH * BS), BF16),
            jax.ShapeDtypeStruct((NZ, PAIRS, QH * 8, 128), BF16),
        ),
        in_specs=[
            SMEM,
            pl.BlockSpec((2, NCLS, NCLS), lambda p: (p, 0, 0)),
            HBM,
            HBM,
            pl.BlockSpec((NX, None, NX * 8, 128), lambda p: (0, p, 0, 0)),
        ],
        out_specs=(
            pl.BlockSpec((2, NCLS * 8, QH * BS), lambda p: (p, 0, 0)),
            pl.BlockSpec((NZ, 1, QH * 8, 128), lambda p: (0, p, 0, 0)),
        ),
        scratch_shapes=[
            pltpu.VMEM((NY, 16, MEM, 8, QH * BS), BF16),
            pltpu.VMEM((NCLS, QH * BS), F32),
            pltpu.SemaphoreType.DMA((4,)),
        ],
    )(mu, mask, own, xg, y)


def second_kernel(chosen_ref, y_ref, out_ref):
    left = y_ref[...].reshape(NCLS * 8, 128).T
    for which in range(2):
        part = contract(left[which * BS : which * BS + BS], chosen_ref[which], 1, 0)
        part = part.reshape(NZ, 2, 4, QH * BS).astype(BF16)
        out_ref[:, :, 0, which] = part


def second_product(chosen, y):
    out = pl.pallas_call(
        second_kernel,
        grid=(PAIRS,),
        out_shape=jax.ShapeDtypeStruct((NZ, 2, PAIRS, 2, 4, QH * BS), BF16),
        in_specs=[
            pl.BlockSpec((2, NCLS * 8, QH * BS), lambda p: (p, 0, 0)),
            pl.BlockSpec((NX, None, NX * 8, 128), lambda p: (0, p, 0, 0)),
        ],
        out_specs=pl.BlockSpec((NZ, 2, 1, 2, 4, QH * BS), lambda p: (0, 0, p, 0, 0, 0)),
    )(chosen, y)
    return out.reshape(NZ * 2, MEM, 4, QH * BS)


def square_kernel(part_ref, yg_ref, held, result, zsend, zrecv, ysend, yrecv):
    layer = lax.axis_index("layer")
    half = lax.rem(layer, 2)
    z = layer // 2
    slot, peers = plane_peers()
    others = [{"layer": lax.rem(z + o, NZ) * 2 + half} for o in range(1, NZ)]
    greet(others + peers)
    sends = []
    for o in (4, 3, 5, 2, 6, 1, 7):
        one = pltpu.make_async_remote_copy(
            src_ref=part_ref.at[lax.rem(z + o, NZ)], dst_ref=held.at[o - 1],
            send_sem=zsend.at[o - 1], recv_sem=zrecv.at[o - 1], device_id=others[o - 1], device_id_type=MESH,
        )
        one.start()
        sends.append(one)
    for one in sends:
        one.wait_recv()
    for p in range(PAIRS):
        total = part_ref[z, p].astype(F32)
        for o in range(NZ - 1):
            total = total + held[o, p].astype(F32)
        result[p] = (SCALE * total).astype(BF16)
    again = []
    for index, peer in enumerate(peers):
        one = pltpu.make_async_remote_copy(
            src_ref=result, dst_ref=yg_ref.at[slot], send_sem=ysend.at[index], recv_sem=yrecv.at[index],
            device_id=peer, device_id_type=MESH,
        )
        one.start()
        again.append(one)
    yg_ref[slot] = result[...]
    for one in sends:
        one.wait_send()
    for one in again:
        one.wait()


def square_sum(part):
    return pl.pallas_call(
        square_kernel,
        out_shape=jax.ShapeDtypeStruct((NX,) + part.shape[1:], BF16),
        in_specs=[VMEM],
        out_specs=VMEM,
        scratch_shapes=[
            pltpu.VMEM((NZ - 1,) + part.shape[1:], BF16),
            pltpu.VMEM(part.shape[1:], BF16),
            pltpu.SemaphoreType.DMA((NZ - 1,)),
            pltpu.SemaphoreType.DMA((NZ - 1,)),
            pltpu.SemaphoreType.DMA((NX - 1,)),
            pltpu.SemaphoreType.DMA((NX - 1,)),
        ],
        compiler_params=pltpu.CompilerParams(collective_id=1, has_side_effects=True),
    )(part)


def cubed_kernel(part_ref, out_ref, held, send, recv):
    layer = lax.axis_index("layer")
    half = lax.rem(layer, 2)
    z = layer // 2
    offsets = [(o, flip) for o in (4, 3, 5, 2, 6, 1, 7, 0) for flip in (1, 0) if o or flip]
    target = {}
    for o, flip in offsets:
        target[o, flip] = lax.rem(z + o, NZ) * 2 + lax.rem(half + flip, 2)
    greet([{"layer": target[key]} for key in offsets])
    sends = []
    for o, flip in offsets:
        index = o * 2 + flip
        one = pltpu.make_async_remote_copy(
            src_ref=part_ref.at[target[o, flip]], dst_ref=held.at[flip, o],
            send_sem=send.at[index], recv_sem=recv.at[index],
            device_id={"layer": target[o, flip]}, device_id_type=MESH,
        )
        one.start()
        sends.append(one)
    for one in sends:
        one.wait_recv()
    for m in range(MEM):
        same = part_ref[layer, m].astype(F32)
        flipped = held[1, 0, m].astype(F32)
        for o in range(1, NZ):
            same = same + held[0, o, m].astype(F32)
            flipped = flipped + held[1, o, m].astype(F32)
        out_ref[half, m] = SCALE * same
        out_ref[1 - half, m] = SCALE * flipped
    for one in sends:
        one.wait_send()


def cubed_sum(part):
    return pl.pallas_call(
        cubed_kernel,
        out_shape=jax.ShapeDtypeStruct((2,) + part.shape[1:], F32),
        in_specs=[VMEM],
        out_specs=VMEM,
        scratch_shapes=[
            pltpu.VMEM((2, NZ) + part.shape[1:], BF16),
            pltpu.SemaphoreType.DMA((2 * NZ,)),
            pltpu.SemaphoreType.DMA((2 * NZ,)),
        ],
        compiler_params=pltpu.CompilerParams(collective_id=2, has_side_effects=True),
    )(part)


def per_device(blocks, grid_class, neighbor):
    heights, window_dev, cols_dev, members, flattened = blocks.shape
    half = lax.rem(lax.axis_index("layer"), 2)
    native = jnp.transpose(blocks[:, 0], (0, 2, 1, 3))
    away = lax.dynamic_slice_in_dim(native, (1 - half) * QH, QH, 2)
    kept = lax.dynamic_slice_in_dim(native, half * QH, QH, 2)
    layers = lax.axis_size("layer")
    came = lax.ppermute(away, "layer", [(l, l ^ 1) for l in range(layers)])
    mu, mask = tables(grid_class, neighbor)

    own = blocks[0, 0]
    cut = own.reshape(2, QH, PAIRS, 2, 4, NZ, 8)
    cut = jnp.transpose(cut, (5, 0, 2, 1, 6, 3, 4)).reshape(layers, PAIRS, QH * 8, 2 * 4)
    cut = lax.all_to_all(cut, "layer", split_axis=0, concat_axis=0, tiled=True)
    cut = cut.reshape(layers, PAIRS, QH * 8, 2, 4)
    left = jnp.transpose(cut, (1, 2, 3, 0, 4)).reshape(PAIRS, QH * 8, 128)

    low = jnp.where(half == 0, kept, came)
    high = jnp.where(half == 0, came, kept)
    both = jnp.stack([low, high], axis=2).reshape(heights, members, 2, QH, 4, BS)
    mine = jnp.transpose(both, (0, 1, 2, 4, 3, 5)).reshape(heights, members, 8, QH * BS)

    xg, yg = gather(mine, left)
    chosen, part = first_product(mu, mask, mine, xg, yg)
    yg = square_sum(part)
    part = second_product(chosen, yg)
    cubed = cubed_sum(part).reshape(2, members, 4, QH, BS)
    cubed = jnp.transpose(cubed, (0, 3, 1, 2, 4)).reshape(cols_dev, members, flattened)
    return (1.5 * own.astype(F32) - 0.5 * cubed).astype(BF16)[None]


def solution(mesh):
    in_specs = (P(None, "col", "row", None, "layer"), P(), P())
    out_specs = P("col", "row", None, "layer")
    return jax.shard_map(
        per_device, mesh=mesh, in_specs=in_specs, out_specs=out_specs, check_vma=False
    )
```

```python
import functools
import math

import jax
import jax.numpy as jnp
from jax import lax
from jax.experimental import pallas as pl
from jax.experimental.pallas import tpu as pltpu
from jax.sharding import PartitionSpec as P

BS = 64
NCLS = 64
WIN = 4
MEM = 12
PAIRS = MEM // 2
NZ = 8
NX = 8
NY = 4
QH = 8
TILES = 16 * MEM
GROUP = 8
CHUNK = QH * BS // 2
GROUPS = 3
PER = PAIRS // GROUPS
SCALE = 1.0 / math.sqrt(NCLS * BS)
MESH = pl.DeviceIdType.MESH
F32 = jnp.float32
BF16 = jnp.bfloat16
VMEM = pl.BlockSpec(memory_space=pltpu.VMEM)
HBM = pl.BlockSpec(memory_space=pl.ANY)
SMEM = pl.BlockSpec(memory_space=pltpu.SMEM)


def contract(a, b, da, db):
    return lax.dot_general(a, b, (((da,), (db,)), ((), ())), preferred_element_type=F32)


def tables_kernel(gcol_ref, neigh_ref, mu_ref, mask_ref, part_ref, col_ref):
    mine = lax.axis_index("col")
    lanes = lax.broadcasted_iota(jnp.int32, (NCLS, NCLS), 1)
    rows = lax.broadcasted_iota(jnp.int32, (NCLS, NCLS), 0)
    place = (gcol_ref[...] == lanes).astype(F32)
    own_row = contract((lax.broadcasted_iota(jnp.int32, (8, NCLS), 1) == mine).astype(F32), place, 1, 0)[0:1]
    for m in range(MEM):
        table = neigh_ref[m].astype(F32)
        half = contract(place, table, 1, 1)
        col_ref[m] = jnp.sum(half * own_row, axis=1, keepdims=True)
        full = contract(place, half, 1, 1)
        part_ref[m] = full
    row_on = rows == mine
    for m in range(MEM):
        target = jnp.sum(jnp.where(row_on, part_ref[m], 0.0), axis=0, keepdims=True)
        mu_ref[m : m + 1, :] = target.astype(jnp.int32)
        column = col_ref[m]
        coupled = jnp.zeros((NCLS, NCLS), F32)
        for other in range(MEM):
            coupled = jnp.where(column == other, part_ref[other], coupled)
        mask_ref[m] = (coupled == target).astype(F32)


def tables(grid_class, neighbor):
    return pl.pallas_call(
        tables_kernel,
        out_shape=(
            jax.ShapeDtypeStruct((MEM, NCLS), jnp.int32),
            jax.ShapeDtypeStruct((MEM, NCLS, NCLS), F32),
        ),
        in_specs=[VMEM, VMEM],
        out_specs=(VMEM, VMEM),
        scratch_shapes=[pltpu.VMEM((MEM, NCLS, NCLS), F32), pltpu.VMEM((MEM, NCLS, 1), F32)],
    )(grid_class[:, None], jnp.transpose(neighbor, (2, 0, 1)))


def greet(peers):
    barrier = pltpu.get_barrier_semaphore()
    for peer in peers:
        pl.semaphore_signal(barrier, inc=1, device_id=peer, device_id_type=MESH)
    pl.semaphore_wait(barrier, len(peers))


def plane_peers():
    row = lax.axis_index("row")
    layer = lax.axis_index("layer")
    half = lax.rem(layer, 2)
    slot = row * 2 + half
    peers = []
    for offset in range(1, NX):
        other = lax.rem(slot + offset, NX)
        peers.append({"row": other // 2, "layer": layer - half + lax.rem(other, 2)})
    return slot, peers


def whole_kernel(
    mu_ref, mask_ref, kept_ref, came_ref, y_ref, out_ref,
    xs0, xs1, stage, merged, spread, chosen, part, held, result, yg1, yg2, part2, held2,
    xsend, xrecv, y1send, y1recv, zsend, zrecv, y2send, y2recv, csend, crecv,
):
    mine = lax.axis_index("col")
    layer = lax.axis_index("layer")
    half = lax.rem(layer, 2)
    z = layer // 2
    right = {"col": lax.rem(mine + 1, NY)}
    left = {"col": lax.rem(mine + NY - 1, NY)}
    slot, peers = plane_peers()
    below = [{"layer": lax.rem(z + o, NZ) * 2 + half} for o in range(1, NZ)]
    ways = [(o, flip) for o in (4, 3, 5, 2, 6, 1, 7, 0) for flip in (1, 0) if o or flip]
    target = {way: lax.rem(z + way[0], NZ) * 2 + lax.rem(half + way[1], 2) for way in ways}
    greet([right, left] + peers + [{"layer": target[way]} for way in ways])

    xs = (xs0, xs1)
    lo, hi = pl.ds(0, TILES // 2), pl.ds(TILES // 2, TILES // 2)

    def xcopy(chunk, index, src, dst, peer):
        return pltpu.make_async_remote_copy(
            src_ref=src, dst_ref=dst, send_sem=xsend.at[chunk, index], recv_sem=xrecv.at[chunk, index],
            device_id=peer, device_id_type=MESH,
        )

    first, forward = [], []
    for c in range(2):
        ref = xs[c]
        first.append([
            xcopy(c, 0, ref.at[0, lo], ref.at[3, lo], right),
            xcopy(c, 1, ref.at[0, hi], ref.at[1, hi], left),
            xcopy(c, 2, ref.at[0, hi], ref.at[3, hi], right),
            xcopy(c, 3, ref.at[0, lo], ref.at[1, lo], left),
        ])
        forward.append([
            xcopy(c, 4, ref.at[3, lo], ref.at[2, lo], right),
            xcopy(c, 5, ref.at[1, hi], ref.at[2, hi], left),
        ])

    y1 = []
    for index, peer in enumerate(peers):
        one = pltpu.make_async_remote_copy(
            src_ref=y_ref, dst_ref=yg1.at[slot], send_sem=y1send.at[index], recv_sem=y1recv.at[index],
            device_id=peer, device_id_type=MESH,
        )
        one.start()
        y1.append(one)
    yg1[slot] = y_ref[...]

    low_lanes = lax.broadcasted_iota(jnp.int32, (GROUP * 4, 128), 1) < BS

    def relay(block, carry):
        base = block * GROUP
        for t in range(GROUP):
            for source, where in ((kept_ref, half), (came_ref, 1 - half)):
                tile = source[base + t].astype(F32)
                for high in range(2):
                    start = pl.multiple_of(t * 32 + where * 16 + high * 8, 8)
                    stage[pl.ds(start, 8), :] = tile[:, high * 128 : high * 128 + 128]
        for pair in range(QH // 2):
            even = stage[pl.ds(2 * pair, GROUP * 4, stride=8), :]
            odd = stage[pl.ds(2 * pair + 1, GROUP * 4, stride=8), :]
            merged[pair, pl.ds(0, GROUP * 4, stride=2), :] = jnp.where(low_lanes, even, pltpu.roll(odd, BS, 1))
            merged[pair, pl.ds(1, GROUP * 4, stride=2), :] = jnp.where(low_lanes, pltpu.roll(even, BS, 1), odd)
        for pair in range(QH // 2):
            tiles = merged[pair].reshape(GROUP, 8, 128).astype(BF16)
            side = pair % 2 * 128
            xs[pair // 2][0, pl.ds(base, GROUP), :, side : side + 128] = tiles
        return carry

    steps = TILES // GROUP
    lax.fori_loop(0, steps // 2, relay, 0)
    first[0][0].start()
    lax.fori_loop(steps // 2, steps, relay, 0)
    for one in first[0][1:]:
        one.start()

    def pass_on(c):
        first[c][0].wait_recv()
        forward[c][0].start()
        first[c][1].wait_recv()
        forward[c][1].start()

    def arrived(c):
        for one in first[c][2:] + forward[c]:
            one.wait_recv()

    base = lax.axis_index("row") * 16 + half * QH
    slots = [lax.rem(w + NY - mine, NY) for w in range(NY)]

    def multiply(c):
        ref = xs[c]
        lane = lax.broadcasted_iota(jnp.int32, (NCLS, CHUNK), 1) // BS
        row = lax.broadcasted_iota(jnp.int32, (NCLS, CHUNK), 0)
        expand = (row == lane + base + c * (QH // 2)).astype(F32)
        columns = pl.ds(c * CHUNK, CHUNK)

        def one_pair(pair, carry):
            for which in range(2):
                m = pair * 2 + which
                spread[which] = contract(mask_ref[m], expand, 1, 0)

                def select(block, inner):
                    for part_h in range(4):
                        h = block * 4 + part_h
                        for w in range(0, NY, 2):
                            a = h * NY + w
                            both = []
                            for more in range(2):
                                tile = ref[slots[w + more], h * MEM + mu_ref[m, a + more]].astype(F32)
                                both.append(tile * spread[which, pl.ds(a + more, 1), :])
                            rows = pl.ds(pl.multiple_of(a * 8, 16), 16)
                            chosen[m, rows, columns] = jnp.concatenate(both, axis=0).astype(BF16)
                    return inner

                lax.fori_loop(0, 4, select, 0)
            factor = yg1[:, :, pair].reshape(NCLS * 8, 128).T
            top = contract(factor[:BS], chosen[pair * 2, :, columns], 1, 0)
            low = contract(factor[BS:], chosen[pair * 2 + 1, :, columns], 1, 0)
            total = jnp.concatenate([top, low], axis=0).T.reshape(QH // 2, NZ, 8, 128)
            for to in range(NZ):
                part[c, to, pair] = total[:, to].reshape(QH * 4, 128).astype(BF16)
            return carry

        lax.fori_loop(0, PAIRS, one_pair, 0)

    def send_sums(c):
        sends = []
        for o in (4, 3, 5, 2, 6, 1, 7):
            one = pltpu.make_async_remote_copy(
                src_ref=part.at[c, lax.rem(z + o, NZ)], dst_ref=held.at[c, o - 1],
                send_sem=zsend.at[c, o - 1], recv_sem=zrecv.at[c, o - 1], device_id=below[o - 1], device_id_type=MESH,
            )
            one.start()
            sends.append(one)
        return sends

    def add_sums(c, sends):
        for one in sends:
            one.wait_recv()

        def one_pair(pair, carry):
            total = part[c, z, pair].astype(F32)
            for o in range(NZ - 1):
                total = total + held[c, o, pair].astype(F32)
            result[c, pair] = (SCALE * total).astype(BF16)
            return carry

        lax.fori_loop(0, PAIRS, one_pair, 0)
        again = []
        for index, peer in enumerate(peers):
            one = pltpu.make_async_remote_copy(
                src_ref=result.at[c], dst_ref=yg2.at[slot, c], send_sem=y2send.at[c, index],
                recv_sem=y2recv.at[c, index], device_id=peer, device_id_type=MESH,
            )
            one.start()
            again.append(one)
        yg2[slot, c] = result[c]
        return again

    pass_on(0)
    for one in first[1]:
        one.start()
    for one in y1:
        one.wait_recv()
    arrived(0)
    multiply(0)
    sums0 = send_sums(0)
    pass_on(1)
    arrived(1)
    multiply(1)
    sums1 = send_sums(1)
    y20 = add_sums(0, sums0)
    y21 = add_sums(1, sums1)
    for one in y20 + y21:
        one.wait_recv()

    last = []
    for group in range(GROUPS):
        def one_pair(pair, carry):
            factor = yg2[:, :, group * PER + pair].reshape(NCLS * 8, 128).T
            for which in range(2):
                m = (group * PER + pair) * 2 + which
                some = contract(factor[which * BS : which * BS + BS], chosen[m], 1, 0)
                part2[group, :, pair * 2 + which] = some.reshape(NZ * 2, 4, QH * BS).astype(BF16)
            return carry

        lax.fori_loop(0, PER, one_pair, 0)
        for way in ways:
            index = way[0] * 2 + way[1]
            one = pltpu.make_async_remote_copy(
                src_ref=part2.at[group, target[way]], dst_ref=held2.at[group, way[1], way[0]],
                send_sem=csend.at[group, index], recv_sem=crecv.at[group, index],
                device_id={"layer": target[way]}, device_id_type=MESH,
            )
            one.start()
            last.append((group, one))
    for group in range(GROUPS):
        for owner, one in last:
            if owner == group:
                one.wait_recv()

        def add(m, carry):
            same = part2[group, layer, m].astype(F32)
            flipped = held2[group, 1, 0, m].astype(F32)
            for o in range(1, NZ):
                same = same + held2[group, 0, o, m].astype(F32)
                flipped = flipped + held2[group, 1, o, m].astype(F32)
            out_ref[half, group * PER * 2 + m] = SCALE * same
            out_ref[1 - half, group * PER * 2 + m] = SCALE * flipped
            return carry

        lax.fori_loop(0, PER * 2, add, 0)
    for c in range(2):
        for one in first[c] + forward[c]:
            one.wait_send()
    for one in y1 + sums0 + sums1 + y20 + y21:
        one.wait_send()
    for owner, one in last:
        one.wait_send()


def whole(mu, mask, kept, came, y):
    dma = pltpu.SemaphoreType.DMA
    return pl.pallas_call(
        whole_kernel,
        out_shape=jax.ShapeDtypeStruct((2, MEM, 4, QH * BS), F32),
        in_specs=[SMEM, VMEM, VMEM, VMEM, VMEM],
        out_specs=VMEM,
        scratch_shapes=[
            pltpu.VMEM((NY, TILES, 8, CHUNK), BF16),
            pltpu.VMEM((NY, TILES, 8, CHUNK), BF16),
            pltpu.VMEM((GROUP * 32, 128), F32),
            pltpu.VMEM((QH // 2, GROUP * 8, 128), F32),
            pltpu.VMEM((2, NCLS, CHUNK), F32),
            pltpu.VMEM((MEM, NCLS * 8, QH * BS), BF16),
            pltpu.VMEM((2, NZ, PAIRS, QH * 4, 128), BF16),
            pltpu.VMEM((2, NZ - 1, PAIRS, QH * 4, 128), BF16),
            pltpu.VMEM((2, PAIRS, QH * 4, 128), BF16),
            pltpu.VMEM((NX, 2, PAIRS, QH * 4, 128), BF16),
            pltpu.VMEM((NX, 2, PAIRS, QH * 4, 128), BF16),
            pltpu.VMEM((GROUPS, NZ * 2, PER * 2, 4, QH * BS), BF16),
            pltpu.VMEM((GROUPS, 2, NZ, PER * 2, 4, QH * BS), BF16),
            dma((2, 6)),
            dma((2, 6)),
            dma((NX - 1,)),
            dma((NX - 1,)),
            dma((2, NZ - 1)),
            dma((2, NZ - 1)),
            dma((2, NX - 1)),
            dma((2, NX - 1)),
            dma((GROUPS, 2 * NZ)),
            dma((GROUPS, 2 * NZ)),
        ],
        compiler_params=pltpu.CompilerParams(collective_id=0, has_side_effects=True),
    )(mu, mask, kept, came, y)


def per_device(blocks, grid_class, neighbor):
    heights, window_dev, cols_dev, members, flattened = blocks.shape
    half = lax.rem(lax.axis_index("layer"), 2)
    native = jnp.transpose(blocks[:, 0], (0, 2, 1, 3))
    away = lax.dynamic_slice_in_dim(native, (1 - half) * QH, QH, 2)
    kept = lax.dynamic_slice_in_dim(native, half * QH, QH, 2)
    layers = lax.axis_size("layer")
    came = lax.ppermute(away, "layer", [(l, l ^ 1) for l in range(layers)])
    mu, mask = tables(grid_class, neighbor)

    own = blocks[0, 0]
    cut = own.reshape(2, QH, PAIRS, 2, 4, NZ, 8)
    cut = jnp.transpose(cut, (5, 0, 2, 1, 6, 3, 4)).reshape(layers, PAIRS, QH * 8, 2 * 4)
    cut = lax.all_to_all(cut, "layer", split_axis=0, concat_axis=0, tiled=True)
    cut = cut.reshape(layers, PAIRS, 2, QH * 4, 2, 4)
    left = jnp.transpose(cut, (2, 1, 3, 4, 0, 5)).reshape(2, PAIRS, QH * 4, 128)

    cubed = whole(mu, mask, kept.reshape(TILES, QH, 256), came.reshape(TILES, QH, 256), left)
    cubed = cubed.reshape(2, members, 4, QH, BS)
    cubed = jnp.transpose(cubed, (0, 3, 1, 2, 4)).reshape(cols_dev, members, flattened)
    return (1.5 * own.astype(F32) - 0.5 * cubed).astype(BF16)[None]


def solution(mesh):
    in_specs = (P(None, "col", "row", None, "layer"), P(), P())
    out_specs = P("col", "row", None, "layer")
    return jax.shard_map(
        per_device, mesh=mesh, in_specs=in_specs, out_specs=out_specs, check_vma=False
    )
```

```python
import functools
import math

import jax
import jax.numpy as jnp
from jax import lax
from jax.experimental import pallas as pl
from jax.experimental.pallas import tpu as pltpu
from jax.sharding import PartitionSpec as P

BS = 64
NCLS = 64
WIN = 4
MEM = 12
PAIRS = MEM // 2
NZ = 8
NX = 8
NY = 4
QH = 8
TILES = 16 * MEM
GROUP = 8
PIECE = TILES // 4
CHUNK = QH * BS // 2
GROUPS = 3
PER = PAIRS // GROUPS
SCALE = 1.0 / math.sqrt(NCLS * BS)
MESH = pl.DeviceIdType.MESH
F32 = jnp.float32
BF16 = jnp.bfloat16
VMEM = pl.BlockSpec(memory_space=pltpu.VMEM)
HBM = pl.BlockSpec(memory_space=pl.ANY)
SMEM = pl.BlockSpec(memory_space=pltpu.SMEM)


def contract(a, b, da, db):
    return lax.dot_general(a, b, (((da,), (db,)), ((), ())), preferred_element_type=F32)


def tables_kernel(gcol_ref, neigh_ref, mu_ref, mask_ref, part_ref, col_ref):
    mine = lax.axis_index("col")
    lanes = lax.broadcasted_iota(jnp.int32, (NCLS, NCLS), 1)
    rows = lax.broadcasted_iota(jnp.int32, (NCLS, NCLS), 0)
    place = (gcol_ref[...] == lanes).astype(F32)
    own_row = contract((lax.broadcasted_iota(jnp.int32, (8, NCLS), 1) == mine).astype(F32), place, 1, 0)[0:1]
    for m in range(MEM):
        table = neigh_ref[m].astype(F32)
        half = contract(place, table, 1, 1)
        col_ref[m] = jnp.sum(half * own_row, axis=1, keepdims=True)
        full = contract(place, half, 1, 1)
        part_ref[m] = full
    row_on = rows == mine
    for m in range(MEM):
        target = jnp.sum(jnp.where(row_on, part_ref[m], 0.0), axis=0, keepdims=True)
        mu_ref[m : m + 1, :] = target.astype(jnp.int32)
        column = col_ref[m]
        coupled = jnp.zeros((NCLS, NCLS), F32)
        for other in range(MEM):
            coupled = jnp.where(column == other, part_ref[other], coupled)
        mask_ref[m] = (coupled == target).astype(F32)


def tables(grid_class, neighbor):
    return pl.pallas_call(
        tables_kernel,
        out_shape=(
            jax.ShapeDtypeStruct((MEM, NCLS), jnp.int32),
            jax.ShapeDtypeStruct((MEM, NCLS, NCLS), F32),
        ),
        in_specs=[VMEM, VMEM],
        out_specs=(VMEM, VMEM),
        scratch_shapes=[pltpu.VMEM((MEM, NCLS, NCLS), F32), pltpu.VMEM((MEM, NCLS, 1), F32)],
    )(grid_class[:, None], jnp.transpose(neighbor, (2, 0, 1)))


def greet(peers):
    barrier = pltpu.get_barrier_semaphore()
    for peer in peers:
        pl.semaphore_signal(barrier, inc=1, device_id=peer, device_id_type=MESH)
    pl.semaphore_wait(barrier, len(peers))


def plane_peers():
    row = lax.axis_index("row")
    layer = lax.axis_index("layer")
    half = lax.rem(layer, 2)
    slot = row * 2 + half
    peers = []
    for offset in range(1, NX):
        other = lax.rem(slot + offset, NX)
        peers.append({"row": other // 2, "layer": layer - half + lax.rem(other, 2)})
    return slot, peers


def whole_kernel(
    mu_ref, mask_ref, x_ref, out_ref,
    own, kept, came, near0, near1, far0, far1, stage, merged, cut, cut_came, cut_stage, factor1,
    spread, chosen, part, held, result, yg1, yg2, part2, held2,
    lsem, esend, erecv, asend, arecv, xsend, xrecv, y1send, y1recv, zsend, zrecv, y2send, y2recv, csend, crecv,
):
    mine = lax.axis_index("col")
    layer = lax.axis_index("layer")
    half = lax.rem(layer, 2)
    z = layer // 2
    right = {"col": lax.rem(mine + 1, NY)}
    left = {"col": lax.rem(mine + NY - 1, NY)}
    slot, peers = plane_peers()
    below = [{"layer": lax.rem(z + o, NZ) * 2 + half} for o in range(1, NZ)]
    ways = [(o, flip) for o in (4, 3, 5, 2, 6, 1, 7, 0) for flip in (1, 0) if o or flip]
    target = {way: lax.rem(z + way[0], NZ) * 2 + lax.rem(half + way[1], 2) for way in ways}

    keep = pl.ds(pl.multiple_of(half * QH, QH), QH)
    away = pl.ds(pl.multiple_of((1 - half) * QH, QH), QH)
    local = [
        pltpu.make_async_copy(x_ref.at[pl.ds(0, MEM)], own, lsem.at[0]),
        pltpu.make_async_copy(x_ref.at[:, keep], kept, lsem.at[1]),
    ]
    for one in local:
        one.start()
    greet([right, left] + peers + [{"layer": target[way]} for way in ways])

    pieces = [pl.ds(i * PIECE, PIECE) for i in range(4)]
    swap = []
    for i in range(4):
        one = pltpu.make_async_remote_copy(
            src_ref=x_ref.at[pieces[i], away], dst_ref=came.at[pieces[i]], send_sem=esend.at[i], recv_sem=erecv.at[i],
            device_id={"layer": target[0, 1]}, device_id_type=MESH,
        )
        one.start()
        swap.append(one)

    local[0].wait()
    rows = own[...].reshape(MEM * 16, 256)
    lane = lax.broadcasted_iota(jnp.int32, (256, 256), 1)
    apart = lax.broadcasted_iota(jnp.int32, (256, 256), 0) - lane // 128 * 8 - lane % 8
    line = lax.broadcasted_iota(jnp.int32, (MEM * 16, 256), 0)
    spot = lax.broadcasted_iota(jnp.int32, (MEM * 16, 256), 1)
    fits = (spot % 128 // 8 == line // 16 % 2 * 8 + line % 8).astype(F32)
    wide = lax.broadcasted_iota(jnp.int32, (16, MEM * 16), 1)
    tall = lax.broadcasted_iota(jnp.int32, (16, MEM * 16), 0)
    gathers = (tall == wide % 16 // 8 * 8 + wide // 32).astype(BF16)

    def cut_step(step, carry):
        row4, zpair = step // 4, step % 4
        pick = (apart == row4 * 64 + zpair * 16).astype(BF16)
        spread_out = contract(rows, pick, 1, 0) * fits
        flat = contract(gathers, spread_out.astype(BF16), 1, 0).astype(BF16)
        for odd in range(2):
            for side in range(2):
                cut[(zpair * 2 + odd) * 2 + side, row4] = flat[side * 8 : side * 8 + 8, odd * 128 : odd * 128 + 128]
        return carry

    lax.fori_loop(0, 16, cut_step, 0)
    cuts = []
    for way in ways:
        index = way[0] * 2 + way[1]
        one = pltpu.make_async_remote_copy(
            src_ref=cut.at[target[way]], dst_ref=cut_came.at[layer], send_sem=asend.at[index], recv_sem=arecv.at[index],
            device_id={"layer": target[way]}, device_id_type=MESH,
        )
        one.start()
        cuts.append(one)
    cut_came[layer] = cut[layer]

    near, far = (near0, near1), (far0, far1)

    def xcopy(chunk, index, src, dst, peer):
        return pltpu.make_async_remote_copy(
            src_ref=src, dst_ref=dst, send_sem=xsend.at[chunk, index], recv_sem=xrecv.at[chunk, index],
            device_id=peer, device_id_type=MESH,
        )

    rightward, leftward, forward = [], [], []
    for c in range(2):
        ref = near[c]
        rightward.append([xcopy(c, i, ref.at[0, pieces[i]], ref.at[2, pieces[i]], right) for i in range(4)])
        leftward.append([xcopy(c, 4 + i, ref.at[0, pieces[i]], ref.at[1, pieces[i]], left) for i in range(4)])
        forward.append(
            [xcopy(c, 8 + i, ref.at[2, pieces[i]], far[c].at[pieces[i]], right) for i in range(2)]
            + [xcopy(c, 8 + i, ref.at[1, pieces[i]], far[c].at[pieces[i]], left) for i in range(2, 4)]
        )

    low_lanes = lax.broadcasted_iota(jnp.int32, (GROUP * 4, 128), 1) < BS

    def relay(block, carry):
        base = block * GROUP
        for t in range(GROUP):
            for source, where in ((kept, half), (came, 1 - half)):
                tile = source[base + t].astype(F32)
                for high in range(2):
                    start = pl.multiple_of(t * 32 + where * 16 + high * 8, 8)
                    stage[pl.ds(start, 8), :] = tile[:, high * 128 : high * 128 + 128]
        for pair in range(QH // 2):
            even = stage[pl.ds(2 * pair, GROUP * 4, stride=8), :]
            odd = stage[pl.ds(2 * pair + 1, GROUP * 4, stride=8), :]
            merged[pair, pl.ds(0, GROUP * 4, stride=2), :] = jnp.where(low_lanes, even, pltpu.roll(odd, BS, 1))
            merged[pair, pl.ds(1, GROUP * 4, stride=2), :] = jnp.where(low_lanes, pltpu.roll(even, BS, 1), odd)
        for pair in range(QH // 2):
            tiles = merged[pair].reshape(GROUP, 8, 128).astype(BF16)
            side = pair % 2 * 128
            near[pair // 2][0, pl.ds(base, GROUP), :, side : side + 128] = tiles
        return carry

    local[1].wait()
    for i in range(4):
        swap[i].wait_recv()
        lax.fori_loop(i * (PIECE // GROUP), (i + 1) * (PIECE // GROUP), relay, 0)
        rightward[0][i].start()
        leftward[0][i].start()

    for one in cuts:
        one.wait_recv()
    cut_stage[...] = cut_came[...].astype(F32).reshape(NZ * 64, 128)
    for p in range(PAIRS):
        turned = cut_stage[pl.ds(p, BS, stride=8), :].T
        both = jnp.concatenate([turned[:BS], turned[BS:]], axis=1).astype(BF16)
        for q in range(QH):
            away_by = lax.rem(q % 4 + NY - mine, NY)
            place = away_by + away_by // 2 * (5 - 2 * away_by)
            factor1[q // 4, place, p] = both[q * 8 : q * 8 + 8]
    y1 = []
    for index, peer in enumerate(peers):
        one = pltpu.make_async_remote_copy(
            src_ref=factor1, dst_ref=yg1.at[slot], send_sem=y1send.at[index], recv_sem=y1recv.at[index],
            device_id=peer, device_id_type=MESH,
        )
        one.start()
        y1.append(one)
    yg1[slot] = factor1[...]

    base = lax.axis_index("row") * 16 + half * QH
    order = [lax.rem(mine + d, NY) for d in (0, 1, 3, 2)]

    def select(c, e, m, block, count, ref):
        columns = pl.ds(c * CHUNK, CHUNK)
        for pair_h in range(0, count, 2):
            h = block * count + pair_h
            both = []
            for more in range(2):
                a = (h + more) * NY + order[e]
                tile = ref[(h + more) * MEM + mu_ref[m, a]].astype(F32)
                both.append(tile * spread[m, pl.ds(a, 1), :])
            at = pl.ds(pl.multiple_of(e * 128 + h * 8, 16), 16)
            chosen[m, at, columns] = jnp.concatenate(both, axis=0).astype(BF16)

    def select_near(c):
        lane = lax.broadcasted_iota(jnp.int32, (NCLS, CHUNK), 1) // BS
        row = lax.broadcasted_iota(jnp.int32, (NCLS, CHUNK), 0)
        expand = (row == lane + base + c * (QH // 2)).astype(F32)

        def one_member(m, carry):
            spread[m] = contract(mask_ref[m], expand, 1, 0)

            def some(block, inner):
                for e in range(3):
                    select(c, e, m, block, 4, near[c].at[e])
                return inner

            return lax.fori_loop(0, 4, some, carry)

        lax.fori_loop(0, MEM, one_member, 0)

    def factor_of(ref, pair):
        return jnp.concatenate([ref[:, :, e, pair].reshape(128, 128) for e in range(4)], axis=0).T

    def multiply(c):
        columns = pl.ds(c * CHUNK, CHUNK)

        def one_pair(pair, carry):
            for which in range(2):
                def some(block, inner):
                    select(c, 3, pair * 2 + which, block, 8, far[c])
                    return inner

                lax.fori_loop(0, 2, some, 0)
            factor = factor_of(yg1, pair)
            top = contract(factor[:BS], chosen[pair * 2, :, columns], 1, 0)
            low = contract(factor[BS:], chosen[pair * 2 + 1, :, columns], 1, 0)
            total = jnp.concatenate([top, low], axis=0).T.reshape(QH // 2, NZ, 8, 128)
            for to in range(NZ):
                part[c, to, pair] = total[:, to].astype(BF16)
            return carry

        lax.fori_loop(0, PAIRS, one_pair, 0)

    def send_sums(c):
        sends = []
        for o in (4, 3, 5, 2, 6, 1, 7):
            one = pltpu.make_async_remote_copy(
                src_ref=part.at[c, lax.rem(z + o, NZ)], dst_ref=held.at[c, o - 1],
                send_sem=zsend.at[c, o - 1], recv_sem=zrecv.at[c, o - 1], device_id=below[o - 1], device_id_type=MESH,
            )
            one.start()
            sends.append(one)
        return sends

    def add_sums(c, sends):
        for one in sends:
            one.wait_recv()

        def one_pair(pair, carry):
            for e in range(4):
                total = part[c, z, pair, order[e]].astype(F32)
                for o in range(NZ - 1):
                    total = total + held[c, o, pair, order[e]].astype(F32)
                result[c, e, pair] = (SCALE * total).astype(BF16)
            return carry

        lax.fori_loop(0, PAIRS, one_pair, 0)
        again = []
        for index, peer in enumerate(peers):
            one = pltpu.make_async_remote_copy(
                src_ref=result.at[c], dst_ref=yg2.at[slot, c], send_sem=y2send.at[c, index],
                recv_sem=y2recv.at[c, index], device_id=peer, device_id_type=MESH,
            )
            one.start()
            again.append(one)
        yg2[slot, c] = result[c]
        return again

    def pass_on(c):
        for i in range(2):
            rightward[c][i].wait_recv()
            forward[c][i].start()
        for i in range(2, 4):
            leftward[c][i].wait_recv()
            forward[c][i].start()

    def near_arrived(c):
        for one in leftward[c][:2] + rightward[c][2:]:
            one.wait_recv()

    def far_arrived(c):
        for one in forward[c]:
            one.wait_recv()

    pass_on(0)
    for i in range(4):
        rightward[1][i].start()
        leftward[1][i].start()
    near_arrived(0)
    select_near(0)
    for one in y1:
        one.wait_recv()
    far_arrived(0)
    multiply(0)
    sums0 = send_sums(0)
    pass_on(1)
    near_arrived(1)
    select_near(1)
    far_arrived(1)
    multiply(1)
    sums1 = send_sums(1)
    y20 = add_sums(0, sums0)
    y21 = add_sums(1, sums1)
    for one in y20 + y21:
        one.wait_recv()

    last = []
    for group in range(GROUPS):
        def one_pair(pair, carry):
            factor = factor_of(yg2, group * PER + pair)
            for which in range(2):
                m = (group * PER + pair) * 2 + which
                some = contract(factor[which * BS : which * BS + BS], chosen[m], 1, 0)
                part2[group, :, pair * 2 + which] = some.reshape(NZ * 2, 4, QH * BS).astype(BF16)
            return carry

        lax.fori_loop(0, PER, one_pair, 0)
        for way in ways:
            index = way[0] * 2 + way[1]
            one = pltpu.make_async_remote_copy(
                src_ref=part2.at[group, target[way]], dst_ref=held2.at[group, way[1], way[0]],
                send_sem=csend.at[group, index], recv_sem=crecv.at[group, index],
                device_id={"layer": target[way]}, device_id_type=MESH,
            )
            one.start()
            last.append((group, one))
    for group in range(GROUPS):
        for owner, one in last:
            if owner == group:
                one.wait_recv()

        def add(m, carry):
            same = part2[group, layer, m].astype(F32)
            flipped = held2[group, 1, 0, m].astype(F32)
            for o in range(1, NZ):
                same = same + held2[group, 0, o, m].astype(F32)
                flipped = flipped + held2[group, 1, o, m].astype(F32)
            out_ref[half, group * PER * 2 + m] = SCALE * same
            out_ref[1 - half, group * PER * 2 + m] = SCALE * flipped
            return carry

        lax.fori_loop(0, PER * 2, add, 0)
    for c in range(2):
        for one in rightward[c] + leftward[c] + forward[c]:
            one.wait_send()
    for one in swap + cuts + y1 + sums0 + sums1 + y20 + y21:
        one.wait_send()
    for owner, one in last:
        one.wait_send()


def whole(mu, mask, x):
    dma = pltpu.SemaphoreType.DMA
    square = (4, PAIRS, 8, 128)
    return pl.pallas_call(
        whole_kernel,
        out_shape=jax.ShapeDtypeStruct((2, MEM, 4, QH * BS), F32),
        in_specs=[SMEM, VMEM, HBM],
        out_specs=VMEM,
        scratch_shapes=[
            pltpu.VMEM((MEM, 16, 256), BF16),
            pltpu.VMEM((TILES, QH, 256), BF16),
            pltpu.VMEM((TILES, QH, 256), BF16),
            pltpu.VMEM((3, TILES, 8, CHUNK), BF16),
            pltpu.VMEM((3, TILES, 8, CHUNK), BF16),
            pltpu.VMEM((TILES, 8, CHUNK), BF16),
            pltpu.VMEM((TILES, 8, CHUNK), BF16),
            pltpu.VMEM((GROUP * 32, 128), F32),
            pltpu.VMEM((QH // 2, GROUP * 8, 128), F32),
            pltpu.VMEM((NZ * 2, 4, 8, 128), BF16),
            pltpu.VMEM((NZ * 2, 4, 8, 128), BF16),
            pltpu.VMEM((NZ * 64, 128), F32),
            pltpu.VMEM((2,) + square, BF16),
            pltpu.VMEM((MEM, NCLS, CHUNK), F32),
            pltpu.VMEM((MEM, NCLS * 8, QH * BS), BF16),
            pltpu.VMEM((2, NZ, PAIRS, QH // 2, 8, 128), BF16),
            pltpu.VMEM((2, NZ - 1, PAIRS, QH // 2, 8, 128), BF16),
            pltpu.VMEM((2,) + square, BF16),
            pltpu.VMEM((NX, 2) + square, BF16),
            pltpu.VMEM((NX, 2) + square, BF16),
            pltpu.VMEM((GROUPS, NZ * 2, PER * 2, 4, QH * BS), BF16),
            pltpu.VMEM((GROUPS, 2, NZ, PER * 2, 4, QH * BS), BF16),
            dma((2,)),
            dma((4,)),
            dma((4,)),
            dma((NZ * 2,)),
            dma((NZ * 2,)),
            dma((2, 12)),
            dma((2, 12)),
            dma((NX - 1,)),
            dma((NX - 1,)),
            dma((2, NZ - 1)),
            dma((2, NZ - 1)),
            dma((2, NX - 1)),
            dma((2, NX - 1)),
            dma((GROUPS, 2 * NZ)),
            dma((GROUPS, 2 * NZ)),
        ],
        compiler_params=pltpu.CompilerParams(collective_id=0, has_side_effects=True),
    )(mu, mask, x)


def per_device(blocks, grid_class, neighbor):
    heights, window_dev, cols_dev, members, flattened = blocks.shape
    native = jnp.transpose(blocks[:, 0], (0, 2, 1, 3)).reshape(TILES, cols_dev, flattened)
    mu, mask = tables(grid_class, neighbor)
    cubed = whole(mu, mask, native).reshape(2, members, 4, QH, BS)
    cubed = jnp.transpose(cubed, (0, 3, 1, 2, 4)).reshape(cols_dev, members, flattened)
    return (1.5 * blocks[0, 0].astype(F32) - 0.5 * cubed).astype(BF16)[None]


def solution(mesh):
    in_specs = (P(None, "col", "row", None, "layer"), P(), P())
    out_specs = P("col", "row", None, "layer")
    return jax.shard_map(
        per_device, mesh=mesh, in_specs=in_specs, out_specs=out_specs, check_vma=False
    )
```
